256 devices in a mesh: dom: 8 (over x, core), mem: 32 (over z, y).
Axes of the slice: x: 4, y: 4, z: 8, core: 2. Of those that a mesh axis runs over, the one named last changes fastest.
Arguments:
- background_trajectories: bfloat16 [512, 786432], P('mem', 'dom'), may hold values from -6 to 6
- jittered_measurement: bfloat16 [512, 786432], P('mem', 'dom'), may hold values from -6 to 6
- measurement_inverse_variance: float32 [786432], P('dom'), may hold values from 0.25 to 4
- measured_point_number: int32 [12288], P('dom'), may hold values from 0 to 64
- adjacent_region_list: int32 [12288, 16], P(('dom', 'mem')), may hold values from 0 to 12287, as said below
- nearby_separation_tier: int32 [12288, 16], P(('dom', 'mem')), may hold values from 0 to 7, as said below
Outputs:
- increment: bfloat16 [512, 786432], P('mem', 'dom')
The draws below stay inside these ranges and needn't reach their ends.
Inputs may be any that keep to these rules, and one draw needn't show every extreme that they name: Cells 0 to measured_point_number[p] - 1 of patch p are the observed ones. `adjacent_region_list`: column 0 of row p is p itself. The other 15 entries are distinct patches (p + o) mod 12288 with 0 < |o| <= 16, and every row holds both o = -16 and o = 16. `nearby_separation_tier`: column 0 is 0; the other columns hold 1 to 7.
All inputs are finite; a program needn't handle non-finite values.
Results may differ from the reference program's by a relative error of at most 0.0059.
Values may be sent and summed in bfloat16 or wider, within the bound.
A program may use at most 128 MiB of HBM per device.

```python
import math
import jax
import jax.numpy as jnp
from jax import lax

MEMBER_TOTAL = 512
PC = 64
REACH = 16
NB = 16
NCLASS = 8
NPATCH = 12288
GRID_POINTS = 786432


def neighbour_table(base_key):
    row_keys = jax.random.split(jax.random.fold_in(base_key, 11), NPATCH)
    inside = jnp.concatenate([jnp.arange(-REACH + 1, 0, dtype=jnp.int32), jnp.arange(1, REACH, dtype=jnp.int32)])

    def one_row(row_key):
        first_key, latter_seed_handle = jax.random.split(row_key)
        chosen = jax.random.permutation(first_key, inside)[:NB - 3]
        offsets = jnp.concatenate([jnp.array([-REACH, REACH], dtype=jnp.int32), chosen])
        offsets = jax.random.permutation(latter_seed_handle, offsets)
        return jnp.concatenate([jnp.zeros((1,), jnp.int32), offsets])
    every_shift_amount = jax.vmap(one_row)(row_keys)
    return (jnp.arange(NPATCH, dtype=jnp.int32)[:, None] + every_shift_amount) % NPATCH


def draw_adjacent_region_list(key, part):
    return neighbour_table(key).astype(jnp.int32)


def draw_nearby_separation_tier(key, part):
    classes = jax.random.randint(jax.random.fold_in(key, 23), (NPATCH, NB - 1), 1, NCLASS, dtype=jnp.int32)
    return jnp.concatenate([jnp.zeros((NPATCH, 1), jnp.int32), classes], axis=1)


def plant(values, own_key, least, largest):
    longest = values.shape.index(max(values.shape))
    spots = []
    for shift in (0, 1):
        where = [jax.random.randint(jax.random.fold_in(own_key, axis), (), 0, length) for axis, length in enumerate(values.shape)]
        where[longest] = (where[longest] + shift) % values.shape[longest]
        spots.append(tuple(where))
    return values.at[spots[0]].set(least).at[spots[1]].set(largest)


def levels(rng, extent, cuts, low, top_value):
    def one(dim, blocks):
        heights = jax.random.uniform(jax.random.fold_in(jax.random.fold_in(rng, 6), dim), (blocks,), jnp.float32, low / len(cuts), top_value / len(cuts))
        return jnp.repeat(jnp.exp(heights), extent[dim] // blocks).reshape((-1,) + (1,) * (len(extent) - dim - 1))

    level = one(*cuts[0])
    for cut in cuts[1:]:
        level = level * one(*cut)
    return level


def bell_draw(rng, shape, width, most, pieces=(), kind=jnp.bfloat16):
    values = width * jax.random.normal(rng, shape, jnp.float32)
    if pieces:
        values = values * levels(rng, shape, pieces, -0.22, 0.18)
    return jnp.clip(values, -most, most).astype(kind)


def setup_inputs(seed: int = 0) -> dict:
    streams_of = jax.random.split(jax.random.key(seed), 7)
    background_trajectories = bell_draw(streams_of[0], (MEMBER_TOTAL, GRID_POINTS), 1.0, 6.0, ((0, 32), (1, 8)))
    jittered_measurement = bell_draw(streams_of[1], (MEMBER_TOTAL, GRID_POINTS), 1.0, 6.0, ((0, 32), (1, 8)))
    measurement_inverse_variance = jnp.clip(jnp.exp(math.log(4.0) - 2.7725887 * jax.random.uniform(streams_of[2], (GRID_POINTS,), jnp.float32) ** levels(streams_of[2], (GRID_POINTS,), ((0, 8),), -0.2, 0.2)), 0.25, 4.0)
    measured_point_number = plant(jax.random.randint(streams_of[3], (NPATCH,), 0, PC + 1), jax.random.fold_in(streams_of[3], 1), 0, PC).astype(jnp.int32)
    adjacent_region_list = draw_adjacent_region_list(jax.random.fold_in(streams_of[6], 71), 0)
    nearby_separation_tier = draw_nearby_separation_tier(jax.random.fold_in(streams_of[6], 71), 0)
    return dict(background_trajectories=background_trajectories, jittered_measurement=jittered_measurement, measurement_inverse_variance=measurement_inverse_variance, measured_point_number=measured_point_number, adjacent_region_list=adjacent_region_list, nearby_separation_tier=nearby_separation_tier)


def gc_taper(taper_cutoff_length):
    return 1.0 - (5.0 / 3.0) * taper_cutoff_length ** 2 + 0.625 * taper_cutoff_length ** 3 + 0.5 * taper_cutoff_length ** 4 - 0.25 * taper_cutoff_length ** 5


def reference(background_trajectories, jittered_measurement, measurement_inverse_variance, measured_point_number, adjacent_region_list, nearby_separation_tier):
    observed = (jnp.arange(PC, dtype=jnp.int32)[None, :] < measured_point_number[:, None]).reshape(-1)
    measurement_gain_factor = jnp.where(observed, measurement_inverse_variance, jnp.float32(0.0))
    departure_residual = (measurement_gain_factor[None, :] * (jittered_measurement.astype(jnp.float32) - background_trajectories.astype(jnp.float32))).astype(jnp.bfloat16)
    sample_mean_state = jnp.mean(background_trajectories.astype(jnp.float32), axis=0)
    random_jitter_draws = (background_trajectories.astype(jnp.float32) - sample_mean_state[None, :]).astype(jnp.bfloat16)
    taper_weight = gc_taper(nearby_separation_tier.astype(jnp.float32) / NCLASS) / (MEMBER_TOTAL - 1)
    perturb_blocks = random_jitter_draws.reshape(MEMBER_TOTAL, NPATCH, PC)
    innov_blocks = departure_residual.reshape(MEMBER_TOTAL, NPATCH, PC)
    block_rows = math.gcd(NPATCH, 64)

    def block_update(first_patch):
        near_ids = lax.dynamic_slice_in_dim(adjacent_region_list, first_patch, block_rows, 0)
        near_weights = lax.dynamic_slice_in_dim(taper_weight, first_patch, block_rows, 0)
        own_cols = lax.dynamic_slice_in_dim(perturb_blocks, first_patch, block_rows, 1)
        near_cols = jnp.take(perturb_blocks, near_ids, axis=1)
        near_innov = jnp.take(innov_blocks, near_ids, axis=1)
        covariance = jnp.einsum("kbc,kbjd->bcjd", own_cols.astype(jnp.float32), near_cols.astype(jnp.float32))
        covariance = (covariance * near_weights[:, None, :, None]).astype(jnp.bfloat16)
        result_block = jnp.einsum("bcjd,kbjd->kbc", covariance.astype(jnp.float32), near_innov.astype(jnp.float32))
        return result_block.astype(jnp.bfloat16)

    starts = jnp.arange(0, NPATCH, block_rows, dtype=jnp.int32)
    blocks = lax.map(block_update, starts)
    return jnp.moveaxis(blocks, 0, 1).reshape(MEMBER_TOTAL, GRID_POINTS)
```

```python
import jax
import jax.numpy as jnp
from jax import lax
from jax.experimental import pallas as pl
from jax.experimental.pallas import tpu as pltpu
from jax.sharding import PartitionSpec as P

PC = 64
REACH = 16
NCLASS = 8
MEMBERS = 512
GROUPS = 32
SHARE = MEMBERS // GROUPS
OWN = 3072
RIM = REACH * PC
WIDE = OWN + 2 * RIM
BLOCK = 4
ROWS = BLOCK * PC
SPAN = ROWS + 2 * RIM
BLOCKS = OWN // ROWS
PART = OWN // 3


def gc_taper(r):
    return 1.0 - 5.0 / 3.0 * r**2 + 0.625 * r**3 + 0.5 * r**4 - 0.25 * r**5


def mult(value, by):
    return pl.multiple_of(value, by)


def kernel(
    b_ref,
    j_ref,
    g_ref,
    w_ref,
    o_ref,
    bsrc,
    isrc,
    bwin,
    iwin,
    pwin,
    cov,
    obuf,
    wtab,
    wexp,
    lsem,
    wsem,
    bs,
    br,
    bcs,
    bcr,
    js,
    jr,
    jcs,
    jcr,
    hbs,
    hbr,
    hjs,
    hjr,
    osend,
    orecv,
):
    d = lax.axis_index("dom")
    m = lax.axis_index("mem")
    x, c = d // 2, d % 2
    z, y = m // 4, m % 4
    half = m // 16
    place = 2 * (m % 16) + c
    has_left = jnp.logical_or(c == 1, y > 0)
    has_right = jnp.logical_or(c == 0, y < 3)

    def loop(start, stop, body):
        def step(i, carry):
            body(i)
            return carry

        lax.fori_loop(start, stop, step, 0)

    def remote(src, dst, send, recv, dom, mem):
        return pltpu.make_async_remote_copy(
            src_ref=src,
            dst_ref=dst,
            send_sem=send,
            recv_sem=recv,
            device_id={"dom": dom, "mem": mem},
            device_id_type=pl.DeviceIdType.MESH,
        )

    load_b = pltpu.make_async_copy(b_ref, bsrc, lsem.at[0])
    load_j = pltpu.make_async_copy(j_ref, isrc, lsem.at[1])
    load_b.start()
    load_j.start()
    barrier = pltpu.get_barrier_semaphore()

    def greet(t):
        other = (c * 32 + m + t) % 64
        pl.semaphore_signal(
            barrier, inc=1, device_id={"dom": 2 * x + other // 32, "mem": other % 32}
        )

    loop(1, 64, greet)

    @pl.when(jnp.logical_and(c == 0, m == 0))
    def _():
        def greet_lower(t):
            pl.semaphore_signal(
                barrier, inc=1, device_id={"dom": 2 * ((x + 3) % 4) + 1, "mem": t}
            )

        loop(0, GROUPS, greet_lower)

    @pl.when(jnp.logical_and(c == 1, m == GROUPS - 1))
    def _():
        def greet_upper(t):
            pl.semaphore_signal(barrier, inc=1, device_id={"dom": 2 * ((x + 1) % 4), "mem": t})

        loop(0, GROUPS, greet_upper)

    load_b.wait()
    load_j.wait()

    def innovation(k):
        cols = pl.ds(mult(k * OWN, OWN), OWN)
        diff = isrc[:, cols].astype(jnp.float32) - bsrc[:, cols].astype(jnp.float32)
        isrc[:, cols] = (g_ref[:, cols] * diff).astype(jnp.bfloat16)

    loop(0, GROUPS, innovation)
    pl.semaphore_wait(barrier, 64)

    row = c * 32 + m
    keep = row == 2 * m + c
    send_w = remote(w_ref, wtab, wsem.at[0], wsem.at[1], 2 * x + row % 2, row // 2)

    @pl.when(jnp.logical_not(keep))
    def _():
        send_w.start()

    @pl.when(keep)
    def _():
        pltpu.make_async_copy(w_ref, wtab, wsem.at[1]).start()

    def target(t):
        i = t // 2
        tz = 4 * c + (z + i // 4) % 4
        ty = (y + i % 4) % 4
        return tz * 4 + ty, t % 2

    def main(src, win, send, recv, t):
        tm, tc = target(t)
        k = 2 * (tm % 16) + tc
        copy = remote(
            src.at[:, pl.ds(mult(k * OWN, OWN), OWN)],
            win.at[pl.ds(mult(SHARE * m, SHARE), SHARE), pl.ds(RIM, OWN)],
            send.at[t],
            recv.at[m],
            2 * x + tc,
            tm,
        )
        return copy, jnp.logical_and(tm == m, tc == c)

    def send_main(src, win, send, recv):
        def body(t):
            copy, mine = main(src, win, send, recv, t)

            @pl.when(jnp.logical_not(mine))
            def _():
                copy.start()

            @pl.when(mine)
            def _():
                pltpu.make_async_copy(
                    src.at[:, pl.ds(mult(place * OWN, OWN), OWN)],
                    win.at[pl.ds(mult(SHARE * m, SHARE), SHARE), pl.ds(RIM, OWN)],
                    recv.at[m],
                ).start()

        return body

    def end_main(src, win, send, recv):
        def body(t):
            copy, mine = main(src, win, send, recv, t)

            @pl.when(jnp.logical_not(mine))
            def _():
                copy.wait_send()

        return body

    def cross(src, win, send, recv, t):
        up = t % 2
        tz = 4 * c + t // 2
        k = 2 * ((4 * tz + 3 * up) % 16) + up
        first = k * OWN + up * (OWN - RIM)
        step = 2 * up - 1
        there = x * 8 + tz + step + 32
        tx = (there // 8) % 4
        tm = 4 * (there % 8) + 3 * (1 - up)
        tc = 1 - up
        from_ = src.at[:, pl.ds(mult(first, RIM), RIM)]
        to = win.at[
            pl.ds(mult(SHARE * m, SHARE), SHARE), pl.ds(mult((1 - up) * (WIDE - RIM), RIM), RIM)
        ]
        copy = remote(from_, to, send.at[t], recv.at[m], 2 * tx + tc, tm)
        mine = jnp.logical_and(jnp.logical_and(tm == m, tc == c), tx == x)
        return copy, mine, from_, to

    def send_cross(src, win, send, recv):
        def body(t):
            copy, mine, from_, to = cross(src, win, send, recv, t)

            @pl.when(jnp.logical_not(mine))
            def _():
                copy.start()

            @pl.when(mine)
            def _():
                pltpu.make_async_copy(from_, to, recv.at[m]).start()

        return body

    def end_cross(src, win, send, recv):
        def body(t):
            copy, mine, _, _ = cross(src, win, send, recv, t)

            @pl.when(jnp.logical_not(mine))
            def _():
                copy.wait_send()

        return body

    def arrive(ref, sem):
        pltpu.make_async_copy(ref, ref, sem).wait()

    def wait_main(win, recv):
        def body(s):
            arrive(
                win.at[pl.ds(mult(SHARE * s, SHARE), SHARE), pl.ds(RIM, OWN)], recv.at[s]
            )

        loop(0, GROUPS, body)

    def rims(win, send, recv):
        right = remote(
            win.at[:, pl.ds(OWN, RIM)], win.at[:, pl.ds(0, RIM)], send.at[0], recv.at[0],
            2 * x + 1 - c, (m + c) % GROUPS,
        )
        left = remote(
            win.at[:, pl.ds(RIM, RIM)], win.at[:, pl.ds(WIDE - RIM, RIM)], send.at[1], recv.at[1],
            2 * x + 1 - c, (m + c + GROUPS - 1) % GROUPS,
        )
        return right, left

    def send_rims(win, send, recv):
        right, left = rims(win, send, recv)

        @pl.when(has_right)
        def _():
            right.start()

        @pl.when(has_left)
        def _():
            left.start()

    def end_rims(win, send, recv):
        right, left = rims(win, send, recv)

        @pl.when(has_right)
        def _():
            right.wait_send()

        @pl.when(has_left)
        def _():
            left.wait_send()

    def wait_rim(win, recv, crossing, side):
        near = has_right if side else has_left
        cols = pl.ds(side * (WIDE - RIM), RIM)

        @pl.when(near)
        def _():
            arrive(win.at[:, cols], recv.at[side])

        @pl.when(jnp.logical_not(near))
        def _():
            def body(s):
                arrive(
                    win.at[pl.ds(mult(SHARE * s, SHARE), SHARE), cols], crossing.at[s]
                )

            loop(0, GROUPS, body)

    loop(0, GROUPS, send_main(b_ref, bwin, bs, br))
    loop(0, 8, send_cross(b_ref, bwin, bcs, bcr))
    loop(0, GROUPS // 2, send_main(isrc, iwin, js, jr))

    arrive(wtab, wsem.at[1])
    pick = (
        lax.broadcasted_iota(jnp.int32, (128, SPAN), 1) // PC
        == lax.broadcasted_iota(jnp.int32, (128, SPAN), 0)
    ).astype(jnp.float32)

    def spread(i):
        wexp[i] = jnp.dot(
            wtab[i], pick, preferred_element_type=jnp.float32, precision=lax.Precision.HIGHEST
        )

    loop(0, BLOCKS, spread)

    wait_main(bwin, br)
    send_rims(bwin, hbs, hbr)
    loop(GROUPS // 2, GROUPS, send_main(isrc, iwin, js, jr))
    loop(0, 8, send_cross(isrc, iwin, jcs, jcr))

    def perturb(i):
        cols = pl.ds(mult(i * 256, 256), 256)
        state = bwin[:, cols].astype(jnp.float32)
        mean = jnp.sum(state, axis=0, keepdims=True) * (1.0 / MEMBERS)
        pwin[:, cols] = (state - mean).astype(jnp.bfloat16)

    def covariance(i):
        own = pwin[:, pl.ds(mult(RIM + i * ROWS, ROWS), ROWS)]
        for part in range(3):
            width = SPAN // 3
            near = pwin[:, pl.ds(mult(i * ROWS + part * width, 256), width)]
            full = lax.dot_general(
                own, near, (((0,), (0,)), ((), ())), preferred_element_type=jnp.float32
            )
            for g in range(BLOCK):
                weight = wexp[i, g : g + 1, part * width : (part + 1) * width]
                cov[i, g * PC : (g + 1) * PC, part * width : (part + 1) * width] = (
                    full[g * PC : (g + 1) * PC] * weight
                ).astype(jnp.bfloat16)

    loop(4, 16, perturb)
    loop(4, 8, covariance)
    wait_rim(bwin, hbr, bcr, 0)
    loop(0, 4, perturb)
    loop(0, 4, covariance)
    wait_rim(bwin, hbr, bcr, 1)
    loop(16, 20, perturb)
    loop(8, 12, covariance)

    wait_main(iwin, jr)
    send_rims(iwin, hjs, hjr)

    def increment(i):
        near = iwin[:, pl.ds(mult(i * ROWS, ROWS), SPAN)]
        result = lax.dot_general(
            near, cov[i], (((1,), (1,)), ((), ())), preferred_element_type=jnp.float32
        )
        obuf[:, pl.ds(mult(i * ROWS, ROWS), ROWS)] = result.astype(jnp.bfloat16)

    def result(q, t):
        tm = ((z + t // 4) % 8) * 4 + (y + t % 4) % 4
        from_ = obuf.at[pl.ds(mult(SHARE * tm, SHARE), SHARE), pl.ds(q * PART, PART)]
        to = o_ref.at[:, pl.ds(mult(place * OWN + q * PART, PART), PART)]
        copy = remote(
            from_, to, osend.at[q, t], orecv.at[q, place], 2 * x + half, tm
        )
        return copy, jnp.logical_and(tm == m, half == c), from_, to

    def send_result(q):
        def body(t):
            copy, mine, from_, to = result(q, t)

            @pl.when(jnp.logical_not(mine))
            def _():
                copy.start()

            @pl.when(mine)
            def _():
                pltpu.make_async_copy(from_, to, orecv.at[q, place]).start()

        loop(0, GROUPS, body)

    def end_result(q):
        def sent(t):
            copy, mine, _, _ = result(q, t)

            @pl.when(jnp.logical_not(mine))
            def _():
                copy.wait_send()

        def arrived(k):
            arrive(o_ref.at[:, pl.ds(mult(k * OWN + q * PART, PART), PART)], orecv.at[q, k])

        loop(0, GROUPS, sent)
        loop(0, GROUPS, arrived)

    loop(4, 8, increment)
    send_result(1)
    wait_rim(iwin, hjr, jcr, 0)
    loop(0, 4, increment)
    send_result(0)
    wait_rim(iwin, hjr, jcr, 1)
    loop(8, 12, increment)
    send_result(2)

    @pl.when(jnp.logical_not(keep))
    def _():
        send_w.wait_send()

    loop(0, GROUPS, end_main(b_ref, bwin, bs, br))
    loop(0, 8, end_cross(b_ref, bwin, bcs, bcr))
    loop(0, GROUPS, end_main(isrc, iwin, js, jr))
    loop(0, 8, end_cross(isrc, iwin, jcs, jcr))
    end_rims(bwin, hbs, hbr)
    end_rims(iwin, hjs, hjr)
    end_result(1)
    end_result(0)
    end_result(2)


def shards(states, measured, precision, counts, near_patches, tiers):
    observed = (jnp.arange(PC, dtype=jnp.int32)[None, :] < counts[:, None]).reshape(1, -1)
    gain = jnp.where(observed, precision[None, :], jnp.float32(0.0))
    patches = near_patches.shape[0]
    total = patches * lax.axis_size("dom") * lax.axis_size("mem")
    local = jnp.arange(patches, dtype=jnp.int32)[:, None]
    own = (lax.axis_index("dom") * lax.axis_size("mem") + lax.axis_index("mem")) * patches + local
    offset = (near_patches - own + total + total // 2) % total - total // 2
    slot = local % BLOCK + REACH + offset
    weight = gc_taper(tiers.astype(jnp.float32) / NCLASS) / (MEMBERS - 1)
    hit = slot[:, :, None] == jnp.arange(128, dtype=jnp.int32)[None, None, :]
    table = jnp.sum(jnp.where(hit, weight[:, :, None], 0.0), axis=1)
    table = jnp.pad(table.reshape(BLOCKS, BLOCK, 128), ((0, 0), (0, 8 - BLOCK), (0, 0)))
    any_spec = pl.BlockSpec(memory_space=pl.ANY)
    dma = pltpu.SemaphoreType.DMA
    bf16 = jnp.bfloat16
    return pl.pallas_call(
        kernel,
        name="increment",
        out_shape=jax.ShapeDtypeStruct(states.shape, bf16),
        in_specs=[
            any_spec,
            any_spec,
            pl.BlockSpec(memory_space=pltpu.VMEM),
            pl.BlockSpec(memory_space=pltpu.VMEM),
        ],
        out_specs=any_spec,
        scratch_shapes=[
            pltpu.VMEM(states.shape, bf16),
            pltpu.VMEM(states.shape, bf16),
            pltpu.VMEM((MEMBERS, WIDE), bf16),
            pltpu.VMEM((MEMBERS, WIDE), bf16),
            pltpu.VMEM((MEMBERS, WIDE), bf16),
            pltpu.VMEM((BLOCKS, ROWS, SPAN), bf16),
            pltpu.VMEM((MEMBERS, OWN), bf16),
            pltpu.VMEM((BLOCKS, 8, 128), jnp.float32),
            pltpu.VMEM((BLOCKS, 8, SPAN), jnp.float32),
            dma((2,)),
            dma((2,)),
            dma((GROUPS,)),
            dma((GROUPS,)),
            dma((8,)),
            dma((GROUPS,)),
            dma((GROUPS,)),
            dma((GROUPS,)),
            dma((8,)),
            dma((GROUPS,)),
            dma((2,)),
            dma((2,)),
            dma((2,)),
            dma((2,)),
            dma((3, GROUPS)),
            dma((3, GROUPS)),
        ],
        compiler_params=pltpu.CompilerParams(
            collective_id=0, has_side_effects=True, vmem_limit_bytes=58 * 1024 * 1024
        ),
    )(states, measured, gain, table)


def solution(mesh):
    in_specs = (
        P("mem", "dom"),
        P("mem", "dom"),
        P("dom"),
        P("dom"),
        P(("dom", "mem"), None),
        P(("dom", "mem"), None),
    )
    return jax.shard_map(
        shards, mesh=mesh, in_specs=in_specs, out_specs=P("mem", "dom"), check_vma=False
    )
```

```python
import jax
import jax.numpy as jnp
from jax import lax
from jax.experimental import pallas as pl
from jax.experimental.pallas import tpu as pltpu
from jax.sharding import PartitionSpec as P

PC = 64
REACH = 16
NCLASS = 8
MEMBERS = 512
GROUPS = 32
SHARE = MEMBERS // GROUPS
OWN = 3072
RIM = REACH * PC
WIDE = OWN + 2 * RIM
BLOCK = 4
ROWS = BLOCK * PC
SPAN = ROWS + 2 * RIM
BLOCKS = OWN // ROWS
TEAM = MEMBERS // 4


def gc_taper(r):
    return 1.0 - 5.0 / 3.0 * r**2 + 0.625 * r**3 + 0.5 * r**4 - 0.25 * r**5


def mult(value, by):
    return pl.multiple_of(value, by)


def kernel(
    b_ref,
    j_ref,
    g_ref,
    n_ref,
    a_ref,
    t_ref,
    o_ref,
    bsrc,
    isrc,
    bwin,
    iwin,
    pwin,
    cov,
    obuf,
    nexp,
    atab,
    ttab,
    wexp,
    lsem,
    wsem,
    bs,
    br,
    bcs,
    bcr,
    js,
    jr,
    jcs,
    jcr,
    hbs,
    hbr,
    hjs,
    hjr,
    osend,
    orecv,
):
    d = lax.axis_index("dom")
    m = lax.axis_index("mem")
    x, c = d // 2, d % 2
    z, y = m // 4, m % 4
    turn = 1 + 2 * (z % 2)
    seat = (z % 4) * 8 + (z // 4) * 4 + y
    half = m // 16
    place = 2 * (m % 16) + c
    has_left = jnp.logical_or(c == 1, y > 0)
    has_right = jnp.logical_or(c == 0, y < 3)

    def loop(start, stop, body):
        def step(i, carry):
            body(i)
            return carry

        lax.fori_loop(start, stop, step, 0)

    def remote(src, dst, send, recv, dom, mem):
        return pltpu.make_async_remote_copy(
            src_ref=src,
            dst_ref=dst,
            send_sem=send,
            recv_sem=recv,
            device_id={"dom": dom, "mem": mem},
            device_id_type=pl.DeviceIdType.MESH,
        )

    load_b = pltpu.make_async_copy(b_ref, bsrc, lsem.at[0])
    load_j = pltpu.make_async_copy(j_ref, isrc, lsem.at[1])
    load_b.start()
    load_j.start()
    barrier = pltpu.get_barrier_semaphore()

    def greet(t):
        other = (c * 32 + m + t) % 64
        pl.semaphore_signal(
            barrier, inc=1, device_id={"dom": 2 * x + other // 32, "mem": other % 32}
        )

    loop(1, 64, greet)

    @pl.when(jnp.logical_and(c == 0, m == 0))
    def _():
        def greet_lower(t):
            pl.semaphore_signal(
                barrier, inc=1, device_id={"dom": 2 * ((x + 3) % 4) + 1, "mem": t}
            )

        loop(0, GROUPS, greet_lower)

    @pl.when(jnp.logical_and(c == 1, m == GROUPS - 1))
    def _():
        def greet_upper(t):
            pl.semaphore_signal(barrier, inc=1, device_id={"dom": 2 * ((x + 1) % 4), "mem": t})

        loop(0, GROUPS, greet_upper)

    pl.semaphore_wait(barrier, 64)

    row = c * 32 + m
    keep = row == 2 * m + c
    send_a = remote(a_ref, atab, wsem.at[0], wsem.at[1], 2 * x + row % 2, row // 2)
    send_t = remote(t_ref, ttab, wsem.at[2], wsem.at[3], 2 * x + row % 2, row // 2)

    def send_lists():
        @pl.when(jnp.logical_not(keep))
        def _():
            send_a.start()
            send_t.start()

        @pl.when(keep)
        def _():
            pltpu.make_async_copy(a_ref, atab, wsem.at[1]).start()
            pltpu.make_async_copy(t_ref, ttab, wsem.at[3]).start()

    def target(t):
        tz = 4 * c + (z + turn * (t // 8)) % 4
        ty = (y + (t // 2) % 4) % 4
        return tz * 4 + ty, t % 2

    def main(src, win, send, recv, t):
        tm, tc = target(t)
        k = 2 * (tm % 16) + tc
        copy = remote(
            src.at[:, pl.ds(mult(k * OWN, OWN), OWN)],
            win.at[pl.ds(mult(SHARE * seat, SHARE), SHARE), pl.ds(RIM, OWN)],
            send.at[t],
            recv.at[seat],
            2 * x + tc,
            tm,
        )
        return copy, jnp.logical_and(tm == m, tc == c)

    def send_main(src, win, send, recv):
        def body(t):
            copy, mine = main(src, win, send, recv, t)

            @pl.when(jnp.logical_not(mine))
            def _():
                copy.start()

            @pl.when(mine)
            def _():
                pltpu.make_async_copy(
                    src.at[:, pl.ds(mult(place * OWN, OWN), OWN)],
                    win.at[pl.ds(mult(SHARE * seat, SHARE), SHARE), pl.ds(RIM, OWN)],
                    recv.at[seat],
                ).start()

        return body

    def end_main(src, win, send, recv):
        def body(t):
            copy, mine = main(src, win, send, recv, t)

            @pl.when(jnp.logical_not(mine))
            def _():
                copy.wait_send()

        return body

    def cross(src, win, send, recv, t):
        up = t % 2
        tz = 4 * c + (z + turn * (t // 2) + 1 + 2 * up) % 4
        k = 2 * ((4 * tz + 3 * up) % 16) + up
        first = k * OWN + up * (OWN - RIM)
        step = 2 * up - 1
        there = x * 8 + tz + step + 32
        tx = (there // 8) % 4
        tm = 4 * (there % 8) + 3 * (1 - up)
        tc = 1 - up
        from_ = src.at[:, pl.ds(mult(first, RIM), RIM)]
        to = win.at[
            pl.ds(mult(SHARE * seat, SHARE), SHARE), pl.ds(mult((1 - up) * (WIDE - RIM), RIM), RIM)
        ]
        copy = remote(from_, to, send.at[t], recv.at[seat], 2 * tx + tc, tm)
        mine = jnp.logical_and(jnp.logical_and(tm == m, tc == c), tx == x)
        return copy, mine, from_, to

    def send_cross(src, win, send, recv):
        def body(t):
            copy, mine, from_, to = cross(src, win, send, recv, t)

            @pl.when(jnp.logical_not(mine))
            def _():
                copy.start()

            @pl.when(mine)
            def _():
                pltpu.make_async_copy(from_, to, recv.at[seat]).start()

        return body

    def end_cross(src, win, send, recv):
        def body(t):
            copy, mine, _, _ = cross(src, win, send, recv, t)

            @pl.when(jnp.logical_not(mine))
            def _():
                copy.wait_send()

        return body

    def arrive(ref, sem):
        pltpu.make_async_copy(ref, ref, sem).wait()

    def wait_main(win, recv, team):
        def body(s):
            arrive(
                win.at[pl.ds(mult(SHARE * s, SHARE), SHARE), pl.ds(RIM, OWN)], recv.at[s]
            )

        loop(team * 8, team * 8 + 8, body)

    def rims(win, send, recv, team):
        rows = pl.ds(mult(team * TEAM, TEAM), TEAM)
        right = remote(
            win.at[rows, pl.ds(OWN, RIM)], win.at[rows, pl.ds(0, RIM)],
            send.at[0, team], recv.at[0, team], 2 * x + 1 - c, (m + c) % GROUPS,
        )
        left = remote(
            win.at[rows, pl.ds(RIM, RIM)], win.at[rows, pl.ds(WIDE - RIM, RIM)],
            send.at[1, team], recv.at[1, team], 2 * x + 1 - c, (m + c + GROUPS - 1) % GROUPS,
        )
        return right, left

    def send_rims(win, send, recv, team):
        right, left = rims(win, send, recv, team)

        @pl.when(has_right)
        def _():
            right.start()

        @pl.when(has_left)
        def _():
            left.start()

    def end_rims(win, send, recv, team):
        right, left = rims(win, send, recv, team)

        @pl.when(has_right)
        def _():
            right.wait_send()

        @pl.when(has_left)
        def _():
            left.wait_send()

    def wait_rim(win, recv, crossing, side, team):
        near = has_right if side else has_left
        cols = pl.ds(side * (WIDE - RIM), RIM)

        @pl.when(near)
        def _():
            arrive(win.at[pl.ds(mult(team * TEAM, TEAM), TEAM), cols], recv.at[side, team])

        @pl.when(jnp.logical_not(near))
        def _():
            def body(s):
                arrive(
                    win.at[pl.ds(mult(SHARE * s, SHARE), SHARE), cols], crossing.at[s]
                )

            loop(team * 8, team * 8 + 8, body)

    def members_out(src, win, send, recv, csend, crecv, phase):
        loop(phase * 8, phase * 8 + 8, send_main(src, win, send, recv))
        loop(phase * 2, phase * 2 + 2, send_cross(src, win, csend, crecv))

    def states_out(phase):
        members_out(b_ref, bwin, bs, br, bcs, bcr, phase)

    def innovations_out(phase):
        members_out(isrc, iwin, js, jr, jcs, jcr, phase)

    def team_of(phase):
        return (z + turn * phase) % 4

    loop(0, 4, states_out)
    send_lists()

    pick_patch = (
        lax.broadcasted_iota(jnp.int32, (48, OWN), 1) // PC
        == lax.broadcasted_iota(jnp.int32, (48, OWN), 0)
    ).astype(jnp.bfloat16)
    counts = n_ref[...].astype(jnp.float32).astype(jnp.bfloat16)
    nexp[...] = jnp.dot(counts, pick_patch, preferred_element_type=jnp.float32)
    cell = (lax.broadcasted_iota(jnp.int32, (1, OWN), 1) % PC).astype(jnp.float32)
    load_b.wait()
    load_j.wait()

    def innovation(k):
        cols = pl.ds(mult(k * OWN, OWN), OWN)
        gain = jnp.where(cell < nexp[pl.ds(k, 1), :], g_ref[:, cols], 0.0)
        diff = isrc[:, cols].astype(jnp.float32) - bsrc[:, cols].astype(jnp.float32)
        isrc[:, cols] = (gain * diff).astype(jnp.bfloat16)

    loop(0, GROUPS, innovation)
    loop(0, 2, innovations_out)

    arrive(atab, wsem.at[1])
    arrive(ttab, wsem.at[3])
    local = lax.broadcasted_iota(jnp.int32, (48, 16), 0)
    offset = atab[...] - ((64 * x + 2 * m + c) * 48 + local)
    total = 256 * 48
    offset = jnp.where(offset > REACH, offset - total, offset)
    offset = jnp.where(offset < -REACH, offset + total, offset)
    slot = local % BLOCK + REACH + offset
    weight = gc_taper(ttab[...].astype(jnp.float32) / NCLASS) / (MEMBERS - 1)
    lane = lax.broadcasted_iota(jnp.int32, (48, 128), 1)
    table = jnp.zeros((48, 128), jnp.float32)
    for j in range(16):
        table = table + jnp.where(lane == slot[:, j : j + 1], weight[:, j : j + 1], 0.0)
    pick = (
        lax.broadcasted_iota(jnp.int32, (128, SPAN), 1) // PC
        == lax.broadcasted_iota(jnp.int32, (128, SPAN), 0)
    ).astype(jnp.float32)
    wide = jnp.dot(
        table, pick, preferred_element_type=jnp.float32, precision=lax.Precision.HIGHEST
    )
    for i in range(BLOCKS):
        wexp[i, 0:BLOCK, :] = wide[i * BLOCK : (i + 1) * BLOCK]

    loop(0, 4, lambda team: wait_main(bwin, br, team))
    loop(0, 4, lambda team: send_rims(bwin, hbs, hbr, team))
    innovations_out(2)

    def perturb(i):
        cols = pl.ds(mult(i * 256, 256), 256)
        state = bwin[:, cols].astype(jnp.float32)
        mean = jnp.sum(state, axis=0, keepdims=True) * (1.0 / MEMBERS)
        pwin[:, cols] = (state - mean).astype(jnp.bfloat16)

    def covariance(i):
        own = pwin[:, pl.ds(mult(RIM + i * ROWS, ROWS), ROWS)]
        for part in range(3):
            width = SPAN // 3
            near = pwin[:, pl.ds(mult(i * ROWS + part * width, 256), width)]
            full = lax.dot_general(
                own, near, (((0,), (0,)), ((), ())), preferred_element_type=jnp.float32
            )
            for g in range(BLOCK):
                weight = wexp[i, g : g + 1, part * width : (part + 1) * width]
                cov[i, g * PC : (g + 1) * PC, part * width : (part + 1) * width] = (
                    full[g * PC : (g + 1) * PC] * weight
                ).astype(jnp.bfloat16)

    def innovations_in(phase):
        team = team_of(phase)
        wait_main(iwin, jr, team)
        send_rims(iwin, hjs, hjr, team)

    def result(team, t):
        s = (y + t) % 4
        tm = (team + 4 * ((z // 4 + t // 4) % 2)) * 4 + s
        tseat = team * 8 + ((z // 4 + t // 4) % 2) * 4 + s
        from_ = obuf.at[pl.ds(mult(SHARE * tseat, SHARE), SHARE), :]
        to = o_ref.at[:, pl.ds(mult(place * OWN, OWN), OWN)]
        copy = remote(from_, to, osend.at[tseat], orecv.at[place], 2 * x + half, tm)
        return copy, jnp.logical_and(tm == m, half == c), from_, to

    def send_result(team):
        def body(t):
            copy, mine, from_, to = result(team, t)

            @pl.when(jnp.logical_not(mine))
            def _():
                copy.start()

            @pl.when(mine)
            def _():
                pltpu.make_async_copy(from_, to, orecv.at[place]).start()

        loop(0, 8, body)

    def end_result(team):
        def sent(t):
            copy, mine, _, _ = result(team, t)

            @pl.when(jnp.logical_not(mine))
            def _():
                copy.wait_send()

        loop(0, 8, sent)

    def increments_out(phase):
        team = team_of(phase)
        rows = pl.ds(mult(team * TEAM, TEAM), TEAM)
        wait_rim(iwin, hjr, jcr, 0, team)
        wait_rim(iwin, hjr, jcr, 1, team)

        def increment(i):
            near = iwin[rows, pl.ds(mult(i * ROWS, ROWS), SPAN)]
            made = lax.dot_general(
                near, cov[i], (((1,), (1,)), ((), ())), preferred_element_type=jnp.float32
            )
            obuf[rows, pl.ds(mult(i * ROWS, ROWS), ROWS)] = made.astype(jnp.bfloat16)

        loop(0, BLOCKS, increment)
        send_result(team)

    loop(4, 16, perturb)
    loop(4, 8, covariance)
    innovations_in(0)
    innovations_out(3)
    loop(0, 4, lambda team: wait_rim(bwin, hbr, bcr, 0, team))
    loop(0, 4, perturb)
    loop(0, 4, covariance)
    loop(0, 4, lambda team: wait_rim(bwin, hbr, bcr, 1, team))
    loop(16, 20, perturb)
    loop(8, 12, covariance)

    def stage(phase):
        innovations_in(phase + 1)
        increments_out(phase)

    loop(0, 3, stage)
    increments_out(3)

    @pl.when(jnp.logical_not(keep))
    def _():
        send_a.wait_send()
        send_t.wait_send()

    loop(0, GROUPS, end_main(b_ref, bwin, bs, br))
    loop(0, 8, end_cross(b_ref, bwin, bcs, bcr))
    loop(0, GROUPS, end_main(isrc, iwin, js, jr))
    loop(0, 8, end_cross(isrc, iwin, jcs, jcr))
    loop(0, 4, lambda team: end_rims(bwin, hbs, hbr, team))
    loop(0, 4, lambda team: end_rims(iwin, hjs, hjr, team))
    loop(0, 4, end_result)
    loop(
        0,
        GROUPS,
        lambda k: arrive(o_ref.at[:, pl.ds(mult(k * OWN, OWN), OWN)], orecv.at[k]),
    )


def shards(states, measured, precision, counts, near_patches, tiers):
    any_spec = pl.BlockSpec(memory_space=pl.ANY)
    dma = pltpu.SemaphoreType.DMA
    bf16 = jnp.bfloat16
    return pl.pallas_call(
        kernel,
        name="increment",
        out_shape=jax.ShapeDtypeStruct(states.shape, bf16),
        in_specs=[
            any_spec,
            any_spec,
            pl.BlockSpec(memory_space=pltpu.VMEM),
            pl.BlockSpec(memory_space=pltpu.VMEM),
            any_spec,
            any_spec,
        ],
        out_specs=any_spec,
        scratch_shapes=[
            pltpu.VMEM(states.shape, bf16),
            pltpu.VMEM(states.shape, bf16),
            pltpu.VMEM((MEMBERS, WIDE), bf16),
            pltpu.VMEM((MEMBERS, WIDE), bf16),
            pltpu.VMEM((MEMBERS, WIDE), bf16),
            pltpu.VMEM((BLOCKS, ROWS, SPAN), bf16),
            pltpu.VMEM((MEMBERS, OWN), bf16),
            pltpu.VMEM((GROUPS, OWN), jnp.float32),
            pltpu.VMEM(near_patches.shape, jnp.int32),
            pltpu.VMEM(near_patches.shape, jnp.int32),
            pltpu.VMEM((BLOCKS, 8, SPAN), jnp.float32),
            dma((2,)),
            dma((4,)),
            dma((GROUPS,)),
            dma((GROUPS,)),
            dma((8,)),
            dma((GROUPS,)),
            dma((GROUPS,)),
            dma((GROUPS,)),
            dma((8,)),
            dma((GROUPS,)),
            dma((2, 4)),
            dma((2, 4)),
            dma((2, 4)),
            dma((2, 4)),
            dma((GROUPS,)),
            dma((GROUPS,)),
        ],
        compiler_params=pltpu.CompilerParams(
            collective_id=0, has_side_effects=True, vmem_limit_bytes=58 * 1024 * 1024
        ),
    )(
        states,
        measured,
        precision.reshape(1, -1),
        counts.reshape(GROUPS, -1),
        near_patches,
        tiers,
    )


def solution(mesh):
    in_specs = (
        P("mem", "dom"),
        P("mem", "dom"),
        P("dom"),
        P("dom"),
        P(("dom", "mem"), None),
        P(("dom", "mem"), None),
    )
    return jax.shard_map(
        shards, mesh=mesh, in_specs=in_specs, out_specs=P("mem", "dom"), check_vma=False
    )
```
